32 devices in a mesh: row: 8 (over y, x, core), col: 4 (over z).
Axes of the slice: x: 2, y: 2, z: 4, core: 2. Of those that a mesh axis runs over, the one named last changes fastest.
Arguments:
- layer_input: bfloat16 [256, 6144], P('row', 'col'), may hold values from -6 to 6
- norm_gain_rows: float32 [2, 6144], P(None, 'col'), may hold values from 0.1 to 1.9
- norm_bias_rows: float32 [2, 6144], P(None, 'col'), may hold values from -3 to 3
- query_key_value_weight: bfloat16 [6144, 3, 6144], P('col', None, 'row'), may hold values from -0.078125 to 0.078125
- adapter_down_maps: bfloat16 [64, 16, 6144], P(None, None, 'col'), may hold values from -0.078125 to 0.078125
- adapter_up_maps: bfloat16 [64, 16, 3, 6144], P(None, None, None, 'row'), may hold values from -6.5 to 6.5
- output_projection: bfloat16 [6144, 6144], P('row', 'col'), may hold values from -0.078125 to 0.078125
- up_projection: bfloat16 [6144, 24576], P('col', 'row'), may hold values from -0.078125 to 0.078125
- down_projection: bfloat16 [24576, 6144], P('row', 'col'), may hold values from -0.0390625 to 0.0390625
- prompt_token_length: int32 [4], replicated, may hold values from 1 to 64, 160 in all
- adapter_index: int32 [4], replicated, may hold values from 0 to 63
- prompt_page_map: int32 [4], replicated, may hold values from 0 to 3, each once
Outputs:
- new_hidden: bfloat16 [256, 6144], P('row', 'col')
- kv_pages: bfloat16 [4, 2, 64, 6144], P('col', None, None, 'row')
The draws below stay inside these ranges and needn't reach their ends.
Inputs may be any that keep to these rules, and one draw needn't show every extreme that they name: `prompt_page_map`: each page is named by exactly one prompt. `prompt_token_length`: the prompts together hold 4 * 64 * 5 // 8 real tokens; some prompt fills all 64 positions.
All inputs are finite; a program needn't handle non-finite values.
Results may differ from the reference program's by a relative error of at most 0.023.
Values may be sent and summed in bfloat16 or wider, within the bound.
A program may use at most 128 MiB of HBM per device.

```python
import math
import jax
import jax.numpy as jnp
import numpy as np
from jax import lax

MODEL_WIDTH = 6144
HEADS = 64
HD = 96
FF = 24576
ROT = 24
ADAPTER_RANK = 16
ADAPTER_COUNT = 64
PLEN = 64
PROMPT_COUNT = 4
TOKENS = 256
N_ROW = 8
N_COL = 4


def draw_layer_input(key, part):
    key_base = jax.random.fold_in(key, 11)
    normal_base = jnp.clip(jax.random.normal(key_base, (TOKENS, MODEL_WIDTH), jnp.float32), -6.0, 6.0)
    return normal_base.astype(jnp.bfloat16)


def draw_adapter_up_maps(key, part):
    key_base = jax.random.fold_in(key, 21)
    normal_base = jax.random.normal(key_base, (ADAPTER_COUNT, ADAPTER_RANK, 3, HEADS * HD), jnp.float32)
    result = jnp.clip(normal_base, -6.0, 6.0) * ADAPTER_RANK ** (-0.5)
    return result.astype(jnp.bfloat16)


def place_ends(array, stream_key, smallest, high):
    longest = array.shape.index(max(array.shape))
    spots = []
    for shift in (0, 1):
        where = [jax.random.randint(jax.random.fold_in(stream_key, axis), (), 0, length) for axis, length in enumerate(array.shape)]
        where[longest] = (where[longest] + shift) % array.shape[longest]
        spots.append(tuple(where))
    return array.at[spots[0]].set(smallest).at[spots[1]].set(high)


def steps_of(key, dims, cuts, least, high):
    level = 1.0
    for dim, blocks in cuts:
        steps = jax.random.uniform(jax.random.fold_in(jax.random.fold_in(key, 6), dim), (blocks,), jnp.float32, least / len(cuts), high / len(cuts))
        level = level * jnp.repeat(jnp.exp(steps), dims[dim] // blocks).reshape((-1,) + (1,) * (len(dims) - 1 - dim))
    return level


def split_up(number_of, total, most, skew):
    portions = [(1 << 20) // math.isqrt(grade ** skew) + 1 for grade in range(2, number_of + 1)]
    spare, counts = total - most - (number_of - 1), [1] * (number_of - 1)
    while spare > 0:
        free = [i for i in range(number_of - 1) if counts[i] < most]
        whole, budget = sum([portions[i] for i in free]), spare
        for i in free:
            addition = min(most - counts[i], max(1, budget * portions[i] // whole), spare)
            counts[i] = counts[i] + addition
            spare = spare - addition
    return np.array([most] + counts)


def uneven(stream_key, number_of, total, limit, slope):
    if number_of == 2:
        one = jax.random.randint(stream_key, (), max(1, total - limit), min(limit, total - 1) + 1)
        return jnp.stack([one, total - one])
    tallies = jnp.asarray(split_up(number_of, total, limit, slope), jnp.int32)
    pairs = (number_of - 1) // 2
    donor, taker = tallies[1:1 + 2 * pairs:2], tallies[2:2 + 2 * pairs:2]
    margin = jnp.minimum(donor - 1, limit - taker)
    moved = jax.random.randint(jax.random.fold_in(stream_key, 1), (pairs,), 0, 1 << 20) % (margin + 1)
    tallies = tallies.at[1:1 + 2 * pairs:2].set(donor - moved).at[2:2 + 2 * pairs:2].set(taker + moved)
    return tallies[jax.random.permutation(jax.random.fold_in(stream_key, 2), number_of)]


def gaussian(key, extent, width, most, shards=(), kind=jnp.bfloat16):
    values = width * jax.random.normal(key, extent, jnp.float32)
    if shards:
        values = values * steps_of(key, extent, shards, -0.22, 0.18)
    return jnp.clip(values, -most, most).astype(kind)


def setup_inputs(seed: int = 0) -> dict:
    seeds = jax.random.split(jax.random.key(seed), 13)
    layer_input = draw_layer_input(jax.random.fold_in(seeds[12], 71), 0)
    norm_gain_rows = jnp.clip(1.0 + 0.18 * jax.random.normal(seeds[1], (2, MODEL_WIDTH), jnp.float32), 0.1, 1.9)
    norm_bias_rows = gaussian(seeds[2], (2, MODEL_WIDTH), 0.5, 3.0, ((1, 4),), jnp.float32)
    query_key_value_weight = gaussian(seeds[3], (MODEL_WIDTH, 3, HEADS * HD), MODEL_WIDTH ** -0.5, 0.078125, ((0, 4), (2, 8)))
    adapter_down_maps = gaussian(seeds[4], (ADAPTER_COUNT, ADAPTER_RANK, MODEL_WIDTH), MODEL_WIDTH ** -0.5, 0.078125, ((2, 4),))
    adapter_up_maps = draw_adapter_up_maps(jax.random.fold_in(seeds[12], 71), 0)
    output_projection = gaussian(seeds[6], (HEADS * HD, MODEL_WIDTH), (HEADS * HD) ** -0.5, 0.078125, ((0, 8), (1, 4)))
    up_projection = gaussian(seeds[7], (MODEL_WIDTH, FF), MODEL_WIDTH ** -0.5, 0.078125, ((0, 4), (1, 8)))
    down_projection = gaussian(seeds[8], (FF, MODEL_WIDTH), FF ** -0.5, 0.0390625, ((0, 8), (1, 4)))
    prompt_token_length = uneven(seeds[9], PROMPT_COUNT, N_COL * PLEN * 5 // 8, PLEN, 2).astype(jnp.int32)
    adapter_index = place_ends(jax.random.randint(seeds[10], (PROMPT_COUNT,), 0, ADAPTER_COUNT), jax.random.fold_in(seeds[10], 1), 0, ADAPTER_COUNT - 1).astype(jnp.int32)
    prompt_page_map = jax.random.permutation(seeds[11], PROMPT_COUNT).astype(jnp.int32)
    return dict(layer_input=layer_input, norm_gain_rows=norm_gain_rows, norm_bias_rows=norm_bias_rows, query_key_value_weight=query_key_value_weight, adapter_down_maps=adapter_down_maps, adapter_up_maps=adapter_up_maps, output_projection=output_projection, up_projection=up_projection, down_projection=down_projection, prompt_token_length=prompt_token_length, adapter_index=adapter_index, prompt_page_map=prompt_page_map)


def norm_rows(hidden_f32, gain_row, bias_row):
    row_mean = lax.optimization_barrier(jnp.sum(hidden_f32, axis=-1, keepdims=True)) / MODEL_WIDTH
    row_var = lax.optimization_barrier(jnp.sum(hidden_f32 * hidden_f32, axis=-1, keepdims=True)) / MODEL_WIDTH - row_mean * row_mean
    return (hidden_f32 - row_mean) * lax.rsqrt(row_var + 1e-05) * gain_row + bias_row

def rotate(heads_in, positions):
    half_rot = ROT // 2
    inv_freq = 10000.0 ** (-jnp.arange(half_rot, dtype=jnp.float32) * 2.0 / ROT)
    angles = positions.astype(jnp.float32)[:, None] * inv_freq[None, :]
    cosine = jnp.cos(angles)[:, None, :]
    sine_part = jnp.sin(angles)[:, None, :]
    front_part = heads_in[..., :half_rot]
    back_part = heads_in[..., half_rot:ROT]
    return jnp.concatenate([front_part * cosine - back_part * sine_part, back_part * cosine + front_part * sine_part, heads_in[..., ROT:]], axis=-1)

def rounded(value):
    return lax.optimization_barrier(value.astype(jnp.bfloat16)).astype(jnp.float32)

def reference(layer_input, norm_gain_rows, norm_bias_rows, query_key_value_weight, adapter_down_maps, adapter_up_maps, output_projection, up_projection, down_projection, prompt_token_length, adapter_index, prompt_page_map):
    hidden_f32 = layer_input.astype(jnp.float32)
    normed_attn = norm_rows(hidden_f32, norm_gain_rows[0], norm_bias_rows[0]).astype(jnp.bfloat16)
    normed_mlp = norm_rows(hidden_f32, norm_gain_rows[1], norm_bias_rows[1]).astype(jnp.bfloat16)
    col_width = MODEL_WIDTH // N_COL
    query_key_value_width = 3 * HEADS * HD
    wide_weight = query_key_value_weight.reshape(MODEL_WIDTH, query_key_value_width)
    selected_down = adapter_down_maps[adapter_index]
    selected_up = adapter_up_maps[adapter_index].reshape(PROMPT_COUNT, ADAPTER_RANK, query_key_value_width)
    qkv_sum = jnp.zeros((TOKENS, query_key_value_width), jnp.float32)
    up_sum = jnp.zeros((TOKENS, FF), jnp.float32)
    for block_index in range(N_COL):
        low_col = block_index * col_width
        piece_attn = normed_attn[:, low_col:low_col + col_width]
        base_term = jnp.dot(piece_attn, wide_weight[low_col:low_col + col_width], preferred_element_type=jnp.float32)
        low_rank = jnp.einsum('pld,prd->plr', piece_attn.reshape(PROMPT_COUNT, PLEN, col_width).astype(jnp.float32), selected_down[:, :, low_col:low_col + col_width].astype(jnp.float32), precision=lax.Precision.HIGHEST).astype(jnp.bfloat16)
        extra_term = jnp.einsum('plr,prk->plk', low_rank.astype(jnp.float32), selected_up.astype(jnp.float32), precision=lax.Precision.HIGHEST).reshape(TOKENS, query_key_value_width)
        qkv_sum = qkv_sum + rounded(base_term + extra_term)
        piece_mlp = normed_mlp[:, low_col:low_col + col_width]
        up_sum = up_sum + rounded(jnp.dot(piece_mlp, up_projection[low_col:low_col + col_width], preferred_element_type=jnp.float32))
    hidden = jax.nn.gelu(up_sum, approximate=False).astype(jnp.bfloat16)
    qkv_sum = qkv_sum.reshape(PROMPT_COUNT, PLEN, 3, HEADS, HD)
    positions = jnp.arange(PLEN, dtype=jnp.int32)
    query = jax.vmap(lambda heads_in: rotate(heads_in, positions))(qkv_sum[:, :, 0]).astype(jnp.bfloat16)
    key_rows = jax.vmap(lambda heads_in: rotate(heads_in, positions))(qkv_sum[:, :, 1]).astype(jnp.bfloat16)
    value_rows = qkv_sum[:, :, 2].astype(jnp.bfloat16)
    live_mask = positions[None, :] < prompt_token_length[:, None]
    zero_key = jnp.zeros_like(key_rows)
    key_rows = jnp.where(live_mask[:, :, None, None], key_rows, zero_key)
    value_rows = jnp.where(live_mask[:, :, None, None], value_rows, zero_key)
    pages_new = jnp.stack([key_rows.reshape(PROMPT_COUNT, PLEN, HEADS * HD), value_rows.reshape(PROMPT_COUNT, PLEN, HEADS * HD)], axis=1)
    kv_pages = jnp.zeros_like(pages_new).at[prompt_page_map].set(pages_new)
    scores = jnp.einsum('pqhe,pkhe->phqk', query.astype(jnp.float32), key_rows.astype(jnp.float32), precision=lax.Precision.HIGHEST) / jnp.sqrt(jnp.float32(HD))
    causal = positions[None, :] <= positions[:, None]
    allowed = causal[None, None, :, :] & live_mask[:, None, None, :]
    scores = jnp.where(allowed, scores, jnp.float32(-1e+30))
    top_score = lax.optimization_barrier(jnp.max(scores, axis=-1, keepdims=True))
    expo = jnp.exp(scores - top_score)
    probs = (expo / lax.optimization_barrier(jnp.sum(expo, axis=-1, keepdims=True))).astype(jnp.bfloat16)
    attended = jnp.einsum('phqk,pkhe->pqhe', probs.astype(jnp.float32), value_rows.astype(jnp.float32), precision=lax.Precision.HIGHEST).astype(jnp.bfloat16)
    attended = attended.reshape(TOKENS, HEADS * HD)
    head_width = HEADS * HD // N_ROW
    unit_width = FF // N_ROW
    branch = jnp.zeros((TOKENS, MODEL_WIDTH), jnp.float32)
    for block_index in range(N_ROW):
        low_head = block_index * head_width
        low_unit = block_index * unit_width
        term_row = jnp.dot(attended[:, low_head:low_head + head_width], output_projection[low_head:low_head + head_width], preferred_element_type=jnp.float32)
        term_row = term_row + jnp.dot(hidden[:, low_unit:low_unit + unit_width], down_projection[low_unit:low_unit + unit_width], preferred_element_type=jnp.float32)
        branch = branch + rounded(term_row)
    new_hidden = (hidden_f32 + branch).astype(jnp.bfloat16)
    return (new_hidden, kv_pages)
```

```python
import functools

import jax
import jax.numpy as jnp
import numpy as np
from jax import lax
from jax.experimental import pallas as pl
from jax.experimental.pallas import tpu as pltpu
from jax.sharding import PartitionSpec as P

MODEL_WIDTH = 6144
HD = 96
ROT = 24


def normalize(hidden_f32, moments, gain_row, bias_row):
    row_mean = (moments[0] / MODEL_WIDTH)[:, None]
    row_var = (moments[1] / MODEL_WIDTH)[:, None] - row_mean * row_mean
    return ((hidden_f32 - row_mean) * lax.rsqrt(row_var + 1e-05) * gain_row + bias_row).astype(
        jnp.bfloat16
    )


def rotate(heads_in, positions):
    half_rot = ROT // 2
    inv_freq = 10000.0 ** (-jnp.arange(half_rot, dtype=jnp.float32) * 2.0 / ROT)
    angles = positions.astype(jnp.float32)[:, None] * inv_freq[None, :]
    cosine = jnp.cos(angles)[:, None, :]
    sine_part = jnp.sin(angles)[:, None, :]
    front_part = heads_in[..., :half_rot]
    back_part = heads_in[..., half_rot:ROT]
    return jnp.concatenate(
        [
            front_part * cosine - back_part * sine_part,
            back_part * cosine + front_part * sine_part,
            heads_in[..., ROT:],
        ],
        axis=-1,
    )


def per_device(
    layer_input,
    norm_gain_rows,
    norm_bias_rows,
    query_key_value_weight,
    adapter_down_maps,
    adapter_up_maps,
    output_projection,
    up_projection,
    down_projection,
    prompt_token_length,
    adapter_index,
    prompt_page_map,
):
    col_width = layer_input.shape[1]
    hidden_f32 = layer_input.astype(jnp.float32)
    moments = lax.psum(
        (jnp.sum(hidden_f32, axis=-1), jnp.sum(hidden_f32 * hidden_f32, axis=-1)), "col"
    )
    normed_attn = normalize(hidden_f32, moments, norm_gain_rows[0], norm_bias_rows[0])
    normed_mlp = normalize(hidden_f32, moments, norm_gain_rows[1], norm_bias_rows[1])
    normed_attn, normed_mlp = (
        lax.all_gather(normed_attn, "row", axis=0, tiled=True),
        lax.all_gather(normed_mlp, "row", axis=0, tiled=True),
    )
    col_count = lax.axis_size("col")
    prompt_span = normed_attn.shape[0] // col_count
    wide_weight = query_key_value_weight.reshape(col_width, -1)
    query_key_value_width = wide_weight.shape[1]
    adapter_wide_term = adapter_up_maps.reshape(
        adapter_up_maps.shape[0], adapter_up_maps.shape[1], query_key_value_width
    )
    slot_index = jnp.arange(col_count, dtype=jnp.int32)
    token_blocks = normed_attn.reshape(col_count, prompt_span, col_width)
    prompt = lax.axis_index("col")
    tok_slice = token_blocks.reshape(lax.axis_size("col") * prompt_span, col_width)
    base_term = jnp.dot(tok_slice, wide_weight, preferred_element_type=jnp.float32)
    selected_adapter = jnp.take(adapter_index, slot_index, axis=0)
    select_down = adapter_down_maps[selected_adapter]
    select_up = adapter_wide_term[selected_adapter]
    low_rank = jnp.einsum(
        "pld,prd->plr", token_blocks, select_down, preferred_element_type=jnp.float32
    ).astype(jnp.bfloat16)
    extra_term = jnp.einsum("plr,prk->plk", low_rank, select_up, preferred_element_type=jnp.float32)
    qkv_rows = lax.psum_scatter(
        (
            base_term
            + extra_term.reshape(lax.axis_size("col") * prompt_span, query_key_value_width)
        ).astype(jnp.bfloat16),
        "col",
        scatter_dimension=0,
        tiled=True,
    ).astype(jnp.float32)
    local_heads = query_key_value_width // (3 * HD)
    qkv_rows = qkv_rows.reshape(prompt_span, 3, local_heads, HD)
    positions = jnp.arange(prompt_span, dtype=jnp.int32)
    prompt_len = lax.dynamic_slice_in_dim(prompt_token_length, prompt, 1, 0)[0]
    live_mask = positions < prompt_len
    query = rotate(qkv_rows[:, 0], positions).astype(jnp.bfloat16)
    key_rows = rotate(qkv_rows[:, 1], positions).astype(jnp.bfloat16)
    value_rows = qkv_rows[:, 2].astype(jnp.bfloat16)
    zero_key = jnp.zeros_like(key_rows)
    key_rows = jnp.where(live_mask[:, None, None], key_rows, zero_key)
    value_rows = jnp.where(live_mask[:, None, None], value_rows, zero_key)
    scores = jnp.einsum(
        "qhe,khe->hqk", query, key_rows, preferred_element_type=jnp.float32
    ) / jnp.sqrt(jnp.float32(HD))
    allowed = (positions[None, :] <= positions[:, None]) & live_mask[None, :]
    scores = jnp.where(allowed[None, :, :], scores, jnp.float32(-1e30))
    top_score = jnp.max(scores, axis=-1, keepdims=True)
    expo = jnp.exp(scores - top_score)
    probs = (expo / jnp.sum(expo, axis=-1, keepdims=True)).astype(jnp.bfloat16)
    attended = jnp.einsum(
        "hqk,khe->qhe", probs, value_rows, preferred_element_type=jnp.float32
    ).astype(jnp.bfloat16)
    attended = attended.reshape(prompt_span, local_heads * HD)
    page_local = jnp.stack(
        [key_rows.reshape(prompt_span, -1), value_rows.reshape(prompt_span, -1)], axis=0
    )[None]
    target_hit = (prompt_page_map == prompt).astype(jnp.bfloat16)
    kv_pages = jnp.einsum(
        "p,pslk->slk",
        target_hit,
        lax.all_gather(page_local, "col", axis=0, tiled=True),
        preferred_element_type=jnp.float32,
    )[None].astype(jnp.bfloat16)
    tok_slice = normed_mlp
    up_rows = lax.psum_scatter(
        jnp.dot(tok_slice, up_projection, preferred_element_type=jnp.float32).astype(jnp.bfloat16),
        "col",
        scatter_dimension=0,
        tiled=True,
    ).astype(jnp.float32)
    hidden = jax.nn.gelu(up_rows, approximate=False).astype(jnp.bfloat16)
    attn_whole, hidden_whole = (
        lax.all_gather(attended, "col", axis=0, tiled=True),
        lax.all_gather(hidden, "col", axis=0, tiled=True),
    )
    branch = lax.psum_scatter(
        (
            jnp.dot(attn_whole, output_projection, preferred_element_type=jnp.float32)
            + jnp.dot(hidden_whole, down_projection, preferred_element_type=jnp.float32)
        ).astype(jnp.bfloat16),
        "row",
        scatter_dimension=0,
        tiled=True,
    ).astype(jnp.float32)
    new_hidden = (layer_input.astype(jnp.float32) + branch).astype(jnp.bfloat16)
    return (new_hidden, kv_pages)


MESH = pl.DeviceIdType.MESH
F32 = jnp.float32
BF16 = jnp.bfloat16


def remote(src, dst, send_sem, recv_sem, device):
    return pltpu.make_async_remote_copy(
        src_ref=src,
        dst_ref=dst,
        send_sem=send_sem,
        recv_sem=recv_sem,
        device_id=device,
        device_id_type=MESH,
    )


def fused_kernel(
    R, C, K, UC, LAG,
    x_ref, gain_ref, bias_ref, wq_hbm, ad_hbm, au_hbm, wo_hbm, wu_hbm, wd_hbm,
    cos_ref, sa_ref, sb_ref, hm_ref, len_ref, aidx_ref, pmap_ref,
    out_ref, kv_ref,
    wq, ad, au, wo, wu, wd,
    xg, mom, momr, st, xn0, xn1, xs, low, qp, rx, qs,
    part, inp, pairb, hid, attb, ao, acc, br, sbuf, cb, rb,
    w_sem, x_send, x_recv, m_send, m_recv, t_send, t_recv, q_send, q_recv,
    p_send, p_recv, h_send, h_recv, a_send, a_recv, s_send, s_recv, b_send, b_recv,
):
    r = lax.axis_index("row")
    c = lax.axis_index("col")
    par = lax.rem(r, 2)
    chip = lax.div(r, 2)
    sib = r + 1 - 2 * par
    H = R // 2
    TR, D = x_ref.shape
    S = (R * TR) // C
    W3 = qs.shape[2]
    per = S // TR

    loads = [
        pltpu.make_async_copy(a, b, w_sem.at[i])
        for i, (a, b) in enumerate(
            [(wq_hbm, wq), (ad_hbm, ad), (au_hbm, au), (wu_hbm, wu), (wo_hbm, wo), (wd_hbm, wd)]
        )
    ]
    for ld in loads:
        ld.start()

    barrier = pltpu.get_barrier_semaphore()
    for i in range(1, R):
        pl.semaphore_signal(barrier, inc=1, device_id={"row": lax.rem(r + i, R)}, device_id_type=MESH)
    for i in range(1, C):
        pl.semaphore_signal(barrier, inc=1, device_id={"col": lax.rem(c + i, C)}, device_id_type=MESH)
    pl.semaphore_wait(barrier, R - 1 + C - 1)

    def x_peer(i):
        return remote(x_ref, xg.at[r], x_send.at[i], x_recv.at[r], {"row": lax.rem(r + 2 * i, R)})

    def x_sib(i):
        src = lax.rem(r + 2 * i, R)
        buf = x_ref if i == 0 else xg.at[src]
        return remote(buf, xg.at[src], x_send.at[H + i], x_recv.at[src], {"row": sib})

    for i in range(1, H):
        x_peer(i).start()
    x_sib(0).start()

    xf = x_ref[...].astype(F32)
    lane = lax.broadcasted_iota(jnp.int32, (TR, 128), 1)
    s1 = jnp.sum(xf, axis=1, keepdims=True)
    s2 = jnp.sum(xf * xf, axis=1, keepdims=True)
    mom[...] = jnp.where(lane == 0, s1, s2)

    def m_peer(i):
        return remote(mom, momr.at[c], m_send.at[i], m_recv.at[c], {"col": lax.rem(c + i, C)})

    def m_from(i):
        src = lax.rem(c + i, C)
        return remote(mom, momr.at[src], m_send.at[i], m_recv.at[src], {"col": src})

    for i in range(1, C):
        m_peer(i).start()
    xg[r] = x_ref[...]
    for i in range(1, C):
        m_from(i).wait_recv()
    tot = mom[...]
    for i in range(1, C):
        tot = tot + momr[lax.rem(c + i, C)]
    st[r] = tot

    def t_peer(i):
        return remote(st.at[r], st.at[r], t_send.at[i], t_recv.at[r], {"row": lax.rem(r + i, R)})

    for i in range(1, R):
        t_peer(i).start()
    for i in range(1, H):
        src = lax.rem(r + 2 * i, R)
        remote(x_ref, xg.at[src], x_send.at[i], x_recv.at[src], {"row": src}).wait_recv()
        x_sib(i).start()

    for src in range(R):
        @pl.when(r != src)
        def _():
            remote(st.at[src], st.at[src], t_send.at[0], t_recv.at[src], {"row": sib}).wait_recv()

        @pl.when(lax.rem(r + src, 2) == 1)
        def _():
            remote(xg.at[src], xg.at[src], x_send.at[0], x_recv.at[src], {"row": sib}).wait_recv()

        mean = st[src][:, 0:1] / MODEL_WIDTH
        var = st[src][:, 1:2] / MODEL_WIDTH - mean * mean
        z = (xg[src].astype(F32) - mean) * lax.rsqrt(var + 1e-05)
        xn0[src // per, pl.ds((src % per) * TR, TR), :] = (z * gain_ref[0:1, :] + bias_ref[0:1, :]).astype(BF16)
        xn1[pl.ds(src * TR, TR), :] = (z * gain_ref[1:2, :] + bias_ref[1:2, :]).astype(BF16)

    inv = []
    for s in range(C):
        v = jnp.int32(0)
        for p in range(1, C):
            v = jnp.where(pmap_ref[p] == s, p, v)
        inv.append(v)
    for s in range(C):
        xs[pl.ds(s * S, S), :] = xn0[inv[s]]
    loads[0].wait()
    loads[1].wait()
    loads[2].wait()
    for s in range(C):
        low[s] = lax.dot_general(
            xs[pl.ds(s * S, S), :], ad[aidx_ref[inv[s]]], (((1,), (1,)), ((), ())),
            preferred_element_type=F32,
        ).astype(BF16)

    def q_right(d, j):
        return remote(qp.at[d, j], rx.at[0, d, j], q_send.at[d, j], q_recv.at[0, d, j], {"col": lax.rem(c + 1, C)})

    def q_left(d, j):
        return remote(qp.at[d, j], rx.at[1, d, j], q_send.at[d, j], q_recv.at[1, d, j], {"col": lax.rem(c + C - 1, C)})

    for j in range(3):
        base = jnp.dot(xs[...], wq[j], preferred_element_type=F32)
        for s in range(C):
            extra = jnp.dot(low[s], au[aidx_ref[inv[s]], j], preferred_element_type=F32)
            qp[s, j] = (base[s * S:(s + 1) * S] + extra).astype(BF16)

        @pl.when(c == 0)
        def _():
            for d in range(C - 1, 0, -1):
                q_right(d, j).start()

        @pl.when(c == C - 1)
        def _():
            for d in range(C - 1):
                q_left(d, j).start()

    loads[3].wait()
    end = jnp.logical_or(c == 0, c == C - 1)
    middle = jnp.logical_not(end)
    inner = jnp.where(c < C // 2, c + 1, c - 1)
    outer = jnp.where(c == 1, 0, C - 1)

    def p_copy(k):
        return remote(part.at[k], inp.at[k], p_send.at[k], p_recv.at[k], {"col": inner})

    def h_copy(k):
        return remote(hid.at[k], hid.at[k], h_send.at[k], h_recv.at[k], {"col": outer})

    def up_term(k):
        cols = pl.ds(pl.multiple_of(k * UC, UC), UC)
        part[k] = jnp.dot(xn1[...], wu[:, cols], preferred_element_type=F32).astype(BF16)

        @pl.when(end)
        def _():
            p_copy(k).start()

    def up_loop(k, carry):
        up_term(k)
        return carry

    lax.fori_loop(0, LAG, up_loop, 0)

    for j in range(3):
        for kk in range(C - 1):
            d = C - 1 - kk

            @pl.when(jnp.logical_and(c > 0, c < d))
            def _():
                q_right(d, j).wait_recv()
                qp[d, j] = (qp[d, j].astype(F32) + rx[0, d, j].astype(F32)).astype(BF16)
                q_right(d, j).start()

            e = kk

            @pl.when(jnp.logical_and(c < C - 1, c > e))
            def _():
                q_left(e, j).wait_recv()
                qp[e, j] = (qp[e, j].astype(F32) + rx[1, e, j].astype(F32)).astype(BF16)
                q_left(e, j).start()

    for j in range(3):
        qs[j] = qp[c, j].astype(F32)

        @pl.when(c > 0)
        def _():
            q_right(c, j).wait_recv()
            qs[j] = qs[j] + rx[0, c, j].astype(F32)

        @pl.when(c < C - 1)
        def _():
            q_left(c, j).wait_recv()
            qs[j] = qs[j] + rx[1, c, j].astype(F32)

    def rot(v):
        return (
            v * cos_ref[...]
            + pltpu.roll(v, W3 - ROT // 2, 1) * sa_ref[...]
            + pltpu.roll(v, ROT // 2, 1) * sb_ref[...]
        )

    mine = jnp.int32(0)
    for p in range(1, C):
        mine = jnp.where(pmap_ref[p] == c, p, mine)
    length = len_ref[mine]
    live = lax.broadcasted_iota(jnp.int32, (S, W3), 0) < length
    query = rot(qs[0]).astype(BF16)
    key = jnp.where(live, rot(qs[1]), 0.0).astype(BF16)
    value = jnp.where(live, qs[2], 0.0).astype(BF16)
    kv_ref[0, 0] = key
    kv_ref[0, 1] = value
    qi = lax.broadcasted_iota(jnp.int32, (S, S), 0)
    ki = lax.broadcasted_iota(jnp.int32, (S, S), 1)
    allowed = jnp.logical_and(ki <= qi, ki < length)
    att = jnp.zeros((S, W3), F32)
    for h in range(W3 // HD):
        mask = hm_ref[h:h + 1, :]
        scores = lax.dot_general(
            query * mask.astype(BF16), key, (((1,), (1,)), ((), ())), preferred_element_type=F32
        ) / np.float32(np.sqrt(np.float32(HD)))
        scores = jnp.where(allowed, scores, -1e30)
        expo = jnp.exp(scores - jnp.max(scores, axis=1, keepdims=True))
        probs = (expo / jnp.sum(expo, axis=1, keepdims=True)).astype(BF16)
        att = att + jnp.dot(probs, value, preferred_element_type=F32) * mask
    attb[c] = att.astype(BF16)

    def a_right(s):
        return remote(attb.at[s], attb.at[s], a_send.at[0, s], a_recv.at[s], {"col": lax.rem(c + 1, C)})

    def a_left(s):
        return remote(attb.at[s], attb.at[s], a_send.at[1, s], a_recv.at[s], {"col": lax.rem(c + C - 1, C)})

    @pl.when(c < C - 1)
    def _():
        a_right(c).start()

    @pl.when(c > 0)
    def _():
        a_left(c).start()

    def att_round(t):
        for s in range(C):
            @pl.when(c == s + t)
            def _():
                a_right(s).wait_recv()
                if s + t < C - 1:
                    a_right(s).start()

            @pl.when(c == s - t)
            def _():
                a_left(s).wait_recv()
                if s - t > 0:
                    a_left(s).start()

    loads[4].wait()
    loads[5].wait()
    acc[...] = jnp.zeros_like(acc)

    def down(k):
        rows = pl.ds(pl.multiple_of(k * UC, UC), UC)
        acc[...] += jnp.dot(hid[k], wd[rows, :], preferred_element_type=F32)

    def main(k, carry):
        @pl.when(k + LAG < K)
        def _():
            up_term(k + LAG)

        @pl.when(jnp.logical_and(middle, k < K))
        def _():
            p_copy(k).wait_recv()
            part[k] = (part[k].astype(F32) + inp[k].astype(F32)).astype(BF16)
            remote(part.at[k], pairb.at[k], p_send.at[k], h_recv.at[k], {"col": inner}).start()

        @pl.when(k >= 1)
        def _():
            m = k - 1

            @pl.when(middle)
            def _():
                remote(part.at[m], pairb.at[m], p_send.at[m], h_recv.at[m], {"col": inner}).wait_recv()
                u = part[m].astype(F32) + pairb[m].astype(F32)
                hid[m] = (0.5 * u * (1.0 + lax.erf(u * np.float32(np.sqrt(0.5))))).astype(BF16)
                h_copy(m).start()

            @pl.when(end)
            def _():
                remote(hid.at[m], hid.at[m], h_send.at[m], h_recv.at[m], {"col": inner}).wait_recv()

            down(m)

        return carry

    bounds = [0] + [K * (t + 1) // (C + 1) + 1 for t in range(1, C)] + [K + 1]
    for t in range(1, C + 1):
        lax.fori_loop(bounds[t - 1], bounds[t], main, 0)
        if t < C:
            att_round(t)
        if t == C - 1:
            for p in range(C):
                ao[pl.ds(p * S, S), :] = attb[pmap_ref[p]]
            acc[...] += jnp.dot(ao[...], wo[...], preferred_element_type=F32)

    for d in range(R):
        br[d] = acc[pl.ds(d * TR, TR), :].astype(BF16)

    def s_copy(i):
        j = lax.rem(chip + i, H)
        return remote(br.at[2 * j + 1 - par], sbuf.at[j], s_send.at[i], s_recv.at[j], {"row": sib})

    def b_copy(i):
        j = lax.rem(chip + i, H)
        return remote(cb.at[j], rb.at[chip], b_send.at[i], b_recv.at[chip], {"row": 2 * j + par})

    def from_sib(i):
        j = lax.rem(chip + i, H)
        remote(sbuf.at[j], sbuf.at[j], s_send.at[i], s_recv.at[j], {"row": sib}).wait_recv()
        return br[2 * j + par].astype(F32) + sbuf[j].astype(F32)

    order = list(range(1, H)) + [0]
    for i in order:
        s_copy(i).start()
    for i in range(1, H):
        cb[lax.rem(chip + i, H)] = from_sib(i).astype(BF16)
        b_copy(i).start()
    total = from_sib(0)
    for i in range(1, H):
        src = lax.rem(chip + i, H)
        remote(cb.at[src], rb.at[src], b_send.at[i], b_recv.at[src], {"row": 2 * src + par}).wait_recv()
        total = total + rb[src].astype(F32)
    out_ref[...] = (x_ref[...].astype(F32) + total).astype(BF16)

    for i in range(1, H):
        x_peer(i).wait_send()
        b_copy(i).wait_send()
    for i in range(H):
        x_sib(i).wait_send()
        s_copy(i).wait_send()
    for i in range(1, C):
        m_peer(i).wait_send()
    for i in range(1, R):
        t_peer(i).wait_send()
    for j in range(3):
        for d in range(C):
            @pl.when(c != d)
            def _():
                q_right(d, j).wait_send()
    for s in range(C):
        @pl.when(jnp.logical_and(s <= c, c < C - 1))
        def _():
            a_right(s).wait_send()

        @pl.when(jnp.logical_and(s >= c, c > 0))
        def _():
            a_left(s).wait_send()

    def drain(k, carry):
        p_copy(k).wait_send()

        @pl.when(middle)
        def _():
            h_copy(k).wait_send()

        return carry

    lax.fori_loop(0, K, drain, 0)


def rotary_tables(span, width):
    half = ROT // 2
    inv_freq = np.float32(10000.0) ** (-np.arange(half, dtype=np.float32) * np.float32(2.0) / np.float32(ROT))
    angles = np.arange(span, dtype=np.float32)[:, None] * inv_freq[None, :].astype(np.float32)
    cosine, sine = np.cos(angles), np.sin(angles)
    cos = np.ones((span, width), np.float32)
    front = np.zeros((span, width), np.float32)
    back = np.zeros((span, width), np.float32)
    for low in range(0, width, HD):
        cos[:, low:low + half] = cosine
        cos[:, low + half:low + ROT] = cosine
        front[:, low:low + half] = -sine
        back[:, low + half:low + ROT] = sine
    heads = (np.arange(width)[None, :] // HD == np.arange(width // HD)[:, None]).astype(np.float32)
    return cos, front, back, heads


def fused(
    layer_input, norm_gain_rows, norm_bias_rows, query_key_value_weight, adapter_down_maps,
    adapter_up_maps, output_projection, up_projection, down_projection, prompt_token_length,
    adapter_index, prompt_page_map,
):
    R, C = lax.axis_size("row"), lax.axis_size("col")
    TR, D = layer_input.shape
    T = TR * R
    S = T // C
    W3 = query_key_value_weight.shape[2]
    U = up_projection.shape[1]
    UC = 256
    K = U // UC
    H = R // 2
    wq = jnp.transpose(query_key_value_weight, (1, 0, 2))
    au = jnp.transpose(adapter_up_maps, (0, 2, 1, 3))
    tables = [jnp.asarray(t) for t in rotary_tables(S, W3)]
    vm = pl.BlockSpec(memory_space=pltpu.VMEM)
    sm = pl.BlockSpec(memory_space=pltpu.SMEM)
    hbm = pl.BlockSpec(memory_space=pl.ANY)
    dma = pltpu.SemaphoreType.DMA
    V = pltpu.VMEM
    return pl.pallas_call(
        functools.partial(fused_kernel, R, C, K, UC, 6),
        out_shape=(
            jax.ShapeDtypeStruct((TR, D), BF16),
            jax.ShapeDtypeStruct((1, 2, S, W3), BF16),
        ),
        in_specs=[vm] * 3 + [hbm] * 6 + [vm] * 4 + [sm] * 3,
        out_specs=(vm, vm),
        scratch_shapes=[
            V(wq.shape, BF16), V(adapter_down_maps.shape, BF16), V(au.shape, BF16),
            V(output_projection.shape, BF16), V(up_projection.shape, BF16), V(down_projection.shape, BF16),
            V((R, TR, D), BF16), V((TR, 128), F32), V((C, TR, 128), F32), V((R, TR, 128), F32),
            V((C, S, D), BF16), V((T, D), BF16), V((T, D), BF16), V((C, S, au.shape[2]), BF16),
            V((C, 3, S, W3), BF16), V((2, C, 3, S, W3), BF16), V((3, S, W3), F32),
            V((K, T, UC), BF16), V((K, T, UC), BF16), V((K, T, UC), BF16), V((K, T, UC), BF16),
            V((C, S, W3), BF16), V((T, W3), BF16), V((T, D), F32),
            V((R, TR, D), BF16), V((H, TR, D), BF16), V((H, TR, D), BF16), V((H, TR, D), BF16),
            dma((6,)), dma((R,)), dma((R,)), dma((C,)), dma((C,)), dma((R,)), dma((R,)),
            dma((C, 3)), dma((2, C, 3)), dma((K,)), dma((K,)), dma((K,)), dma((K,)),
            dma((2, C)), dma((C,)), dma((H,)), dma((H,)), dma((H,)), dma((H,)),
        ],
        compiler_params=pltpu.CompilerParams(
            collective_id=0, has_side_effects=True, vmem_limit_bytes=63 * 1024 * 1024
        ),
    )(
        layer_input, norm_gain_rows, norm_bias_rows, wq, adapter_down_maps, au,
        output_projection, up_projection, down_projection, *tables,
        prompt_token_length, adapter_index, prompt_page_map,
    )


def layer(*args):
    weight, up = args[3], args[7]
    fits = lax.axis_size("col") == 4 and weight.shape[2] % 128 == 0 and up.shape[1] % 256 == 0
    return fused(*args) if fits and weight.shape[0] % 128 == 0 else per_device(*args)


def solution(mesh):
    return jax.shard_map(
        layer,
        mesh=mesh,
        in_specs=(
            P("row", "col"),
            P(None, "col"),
            P(None, "col"),
            P("col", None, "row"),
            P(None, None, "col"),
            P(None, None, None, "row"),
            P("row", "col"),
            P("col", "row"),
            P("row", "col"),
            P(),
            P(),
            P(),
        ),
        out_specs=(P("row", "col"), P("col", None, None, "row")),
        check_vma=False,
    )
```
